32 devices in a mesh: leaf: 8 (over y, x, core), panel: 4 (over z).
Axes of the slice: x: 2, y: 2, z: 4, core: 2. Of those that a mesh axis runs over, the one named last changes fastest.
Arguments:
- live_tiles: int32 [15], replicated, may hold values from 8 to 16
- row_tiles: int32 [14, 8], replicated, may hold values from 0 to 47, as said below
- rhs0: float32 [256, 16384], P('panel', 'leaf'), may hold values from -6 to 6
- rhs1: float32 [256, 8192], P('panel', 'leaf'), may hold values from -6 to 6
- rhs2: float32 [256, 4096], P('panel', 'leaf'), may hold values from -6 to 6
- rhs3: float32 [256, 2048], P('panel', 'leaf'), may hold values from -6 to 6
- dinv0: float32 [16384, 2048], P('leaf', 'panel'), as said below
- dinv1: float32 [8192, 2048], P('leaf', 'panel'), as said below
- dinv2: float32 [4096, 2048], P('leaf', 'panel'), as said below
- dinv3: float32 [2048, 2048], P('leaf', 'panel'), as said below
- off0: float32 [8192, 2048], P('leaf', 'panel'), may hold values from -0.125 to 0.125
- off1: float32 [4096, 2048], P('leaf', 'panel'), may hold values from -0.125 to 0.125
- off2: float32 [2048, 2048], P('leaf', 'panel'), may hold values from -0.125 to 0.125
Outputs:
- sol0: float32 [256, 16384], P('panel', 'leaf')
- sol1: float32 [256, 8192], P('panel', 'leaf')
- sol2: float32 [256, 4096], P('panel', 'leaf')
- sol3: float32 [256, 2048], P('panel', 'leaf')
The draws below stay inside these ranges and needn't reach their ends.
Inputs may be any that keep to these rules, and one draw needn't show every extreme that they name: `row_tiles`: each row names 8 different tiles; for a supernode of level k every value is below (3 - k) * 16. `live_tiles`: counted level by level in the supernodes' order. `dinv0`: each 2048 x 2048 row block is lower triangular with diagonal entries from 0.5 to 2. `dinv1`: each 2048 x 2048 row block is lower triangular with diagonal entries from 0.5 to 2. `dinv2`: each 2048 x 2048 row block is lower triangular with diagonal entries from 0.5 to 2. `dinv3`: each 2048 x 2048 row block is lower triangular with diagonal entries from 0.5 to 2.
All inputs are finite; a program needn't handle non-finite values.
Results may differ from the reference program's by a relative error of at most 0.00028.
Values sent between devices are 32-bit elements; how exact they have to be, the bound alone decides.
A program may use at most 64 MiB of HBM per device.

```python
import math
import jax
import jax.numpy as jnp
from jax import lax

B = 128
NT = 16
ORDER = 2048
RT = 8
R = 256
LEVELS = 4
NODES0 = 8
NODES1 = 4
NODES2 = 2
NODES3 = 1
NODES_ALL = 15


def lower_inverse(key, number):
    row_pos = (jnp.arange(number * ORDER, dtype=jnp.int32) % ORDER)[:, None]
    col_pos = jnp.arange(ORDER, dtype=jnp.int32)[None, :]
    first_key, second_key = jax.random.split(jax.random.fold_in(key, 91))
    spread = jax.random.normal(first_key, (number * ORDER, ORDER), jnp.float32)
    diagonal = jax.random.uniform(second_key, (number * ORDER, 1), jnp.float32, 0.6, 1.6)
    below_diagonal = (col_pos < row_pos).astype(jnp.float32)
    on_diagonal = (col_pos == row_pos).astype(jnp.float32)
    return below_diagonal * spread * (0.6 / math.sqrt(ORDER)) + on_diagonal * diagonal


def draw_dinv0(key, part):
    return lower_inverse(key, NODES0)


def draw_dinv1(key, part):
    return lower_inverse(key, NODES1)


def draw_dinv2(key, part):
    return lower_inverse(key, NODES2)


def draw_dinv3(key, part):
    return lower_inverse(key, NODES3)


def draw_row_tiles(key, part):
    numbers = [NODES0, NODES1, NODES2]
    row_list = []
    for height in range(LEVELS - 1):
        span = (LEVELS - 1 - height) * NT
        node_keys = jax.random.split(jax.random.fold_in(key, 17 + height), numbers[height])
        chosen = jax.vmap(lambda node_key: jax.random.permutation(node_key, span)[:RT])(node_keys)
        row_list.append(chosen.astype(jnp.int32))
    return jnp.concatenate(row_list, 0)


def place_ends(values, stream_key, smallest, high):
    longest = values.shape.index(max(values.shape))
    spots = []
    for shift in (0, 1):
        where = [jax.random.randint(jax.random.fold_in(stream_key, axis), (), 0, length) for axis, length in enumerate(values.shape)]
        where[longest] = (where[longest] + shift) % values.shape[longest]
        spots.append(tuple(where))
    return values.at[spots[0]].set(smallest).at[spots[1]].set(high)


def levels(rng, extent, shards, least, largest):
    level = 1.0
    for dim, shards_of in shards:
        steps = jax.random.uniform(jax.random.fold_in(jax.random.fold_in(rng, 6), dim), (shards_of,), jnp.float32, least / len(shards), largest / len(shards))
        level = level * jnp.repeat(jnp.exp(steps), extent[dim] // shards_of).reshape((-1,) + (1,) * (len(extent) - 1 - dim))
    return level


def centred(own_key, extent, scale, most, shards=(), held_as=jnp.bfloat16):
    values = jax.random.normal(own_key, extent, jnp.float32) * scale
    if len(shards) > 0:
        values = levels(own_key, extent, shards, -0.22, 0.18) * values
    return jnp.clip(values, min=-most, max=most).astype(held_as)


def setup_inputs(seed: int = 0) -> dict:
    arg_keys = jax.random.split(jax.random.key(seed), 14)
    return {
        "live_tiles": place_ends(jax.random.randint(arg_keys[0], (NODES_ALL,), NT // 2, NT + 1), jax.random.fold_in(arg_keys[0], 1), NT // 2, NT).astype(jnp.int32),
        "row_tiles": draw_row_tiles(jax.random.fold_in(arg_keys[13], 71), 0),
        "rhs0": centred(arg_keys[2], (R, NODES0 * ORDER), 1.0, 6.0, ((0, 4), (1, 8)), jnp.float32),
        "rhs1": centred(arg_keys[3], (R, NODES1 * ORDER), 1.0, 6.0, ((0, 4), (1, 8)), jnp.float32),
        "rhs2": centred(arg_keys[4], (R, NODES2 * ORDER), 1.0, 6.0, ((0, 4), (1, 8)), jnp.float32),
        "rhs3": centred(arg_keys[5], (R, NODES3 * ORDER), 1.0, 6.0, ((0, 4), (1, 8)), jnp.float32),
        "dinv0": draw_dinv0(jax.random.fold_in(arg_keys[13], 71), 0),
        "dinv1": draw_dinv1(jax.random.fold_in(arg_keys[13], 71), 0),
        "dinv2": draw_dinv2(jax.random.fold_in(arg_keys[13], 71), 0),
        "dinv3": draw_dinv3(jax.random.fold_in(arg_keys[13], 71), 0),
        "off0": centred(arg_keys[10], (NODES0 * RT * B, ORDER), ORDER ** -0.5, 0.125, ((0, 8), (1, 4)), jnp.float32),
        "off1": centred(arg_keys[11], (NODES1 * RT * B, ORDER), ORDER ** -0.5, 0.125, ((0, 8), (1, 4)), jnp.float32),
        "off2": centred(arg_keys[12], (NODES2 * RT * B, ORDER), ORDER ** -0.5, 0.125, ((0, 8), (1, 4)), jnp.float32),
    }


highest = lax.Precision.HIGHEST


def selector(targets, offset):
    return (targets[:, :, None] == offset + jnp.arange(NT, dtype=jnp.int32)[None, None, :]).astype(jnp.float32)


def reference(live_tiles, row_tiles, rhs0, rhs1, rhs2, rhs3, dinv0, dinv1, dinv2, dinv3, off0, off1, off2):
    right_sides = [rhs0, rhs1, rhs2, rhs3]
    inverses = [dinv0, dinv1, dinv2, dinv3]
    off_rows = [off0, off1, off2]
    counts = [NODES0, NODES1, NODES2, NODES3]
    starts = [0, NODES0, NODES0 + NODES1, NODES0 + NODES1 + NODES2]
    updates = [jnp.zeros((counts[height], R, ORDER), jnp.float32) for height in range(LEVELS)]
    solved = []
    row_masks = []
    for height in range(LEVELS):
        number = counts[height]
        live_count = live_tiles[starts[height]:starts[height] + number]
        row_mask = (jnp.arange(ORDER, dtype=jnp.int32)[None, :] < live_count[:, None] * B).astype(jnp.float32)[:, None, :]
        right = right_sides[height].reshape(R, number, ORDER).transpose(1, 0, 2) - updates[height]
        inverse = inverses[height].reshape(number, ORDER, ORDER)
        result = row_mask * jnp.einsum("nrc,nic->nri", row_mask * right, inverse, precision=highest)
        solved.append(result)
        row_masks.append(row_mask)
        if height < LEVELS - 1:
            blocks = off_rows[height].reshape(number, RT, B, ORDER)
            update = jnp.einsum("nrc,ntbc->ntrb", result, blocks, precision=highest)
            targets = row_tiles[starts[height]:starts[height] + number]
            for ancestor in range(height + 1, LEVELS):
                picked = selector(targets, (ancestor - height - 1) * NT)
                contribution = jnp.einsum("ntrb,ntc->nrcb", update, picked, precision=highest).reshape(number, R, ORDER)
                group_size = 2 ** (ancestor - height)
                updates[ancestor] = updates[ancestor] + contribution.reshape(counts[ancestor], group_size, R, ORDER).sum(1)
    finals = [None] * LEVELS
    for height in reversed(range(LEVELS)):
        number = counts[height]
        result = solved[height]
        if height < LEVELS - 1:
            blocks = off_rows[height].reshape(number, RT * B, ORDER)
            targets = row_tiles[starts[height]:starts[height] + number]
            gathered = jnp.zeros((number, R, RT, B), jnp.float32)
            for ancestor in range(height + 1, LEVELS):
                picked = selector(targets, (ancestor - height - 1) * NT)
                ancestor_x = jnp.repeat(finals[ancestor], 2 ** (ancestor - height), axis=0).reshape(number, R, NT, B)
                gathered = gathered + jnp.einsum("nrcb,ntc->nrtb", ancestor_x, picked, precision=highest)
            result = result - jnp.einsum("nrk,nkc->nrc", gathered.reshape(number, R, RT * B), blocks, precision=highest)
        inverse = inverses[height].reshape(number, ORDER, ORDER)
        finals[height] = row_masks[height] * jnp.einsum("nri,nic->nrc", row_masks[height] * result, inverse, precision=highest)
    return (finals[0].transpose(1, 0, 2).reshape(R, NODES0 * ORDER),
            finals[1].transpose(1, 0, 2).reshape(R, NODES1 * ORDER),
            finals[2].transpose(1, 0, 2).reshape(R, NODES2 * ORDER),
            finals[3].transpose(1, 0, 2).reshape(R, NODES3 * ORDER))
```

```python
import jax
import jax.numpy as jnp
from jax import lax
from jax.experimental import pallas as pl
from jax.experimental.pallas import tpu as pltpu
from jax.sharding import PartitionSpec as P

B = 128
LEVELS = 4

high = lax.Precision.HIGH


def swapped(block, bit):
    count = lax.axis_size("leaf")
    route = [(low, low ^ (1 << bit)) for low in range(count)]
    return lax.ppermute(block, "leaf", route)


def pair(is_lower, mine, other, axis):
    return jnp.where(
        is_lower, jnp.concatenate([mine, other], axis), jnp.concatenate([other, mine], axis)
    )


def pick_half(array, which, axis):
    half = array.shape[axis] // 2
    return lax.dynamic_slice_in_dim(array, which * half, half, axis)


def contract_last(left, right):
    return lax.dot_general(
        left, right, (((1,), (1,)), ((), ())), precision=high, preferred_element_type=jnp.float32
    )


def product(left, right):
    return jnp.dot(left, right, precision=high, preferred_element_type=jnp.float32)


class Panel:
    def __init__(self):
        self.count = lax.axis_size("panel")
        self.calls = 0

    def exchange(self, block, out_shape, source, target, summed):
        count = self.count
        self.calls += 1

        def kernel(x_ref, o_ref, *rest):
            if summed:
                held, send_sems, recv_sems = rest
            else:
                held, (send_sems, recv_sems, local_sem) = o_ref, rest
            me = lax.axis_index("panel")
            barrier = pltpu.get_barrier_semaphore()
            for step in range(1, count):
                pl.semaphore_signal(
                    barrier,
                    inc=1,
                    device_id={"panel": lax.rem(me + step, count)},
                    device_id_type=pl.DeviceIdType.MESH,
                )
            if not summed:
                own = pltpu.make_async_copy(source(x_ref, me), target(held, me), local_sem)
                own.start()
            pl.semaphore_wait(barrier, count - 1)
            copies = []
            for step in sorted(range(1, count), key=lambda s: -min(s, count - s)):
                peer = lax.rem(me + step, count)
                copy = pltpu.make_async_remote_copy(
                    src_ref=source(x_ref, peer),
                    dst_ref=held.at[step - 1] if summed else target(held, me),
                    send_sem=send_sems.at[step - 1],
                    recv_sem=recv_sems.at[step - 1],
                    device_id={"panel": peer},
                    device_id_type=pl.DeviceIdType.MESH,
                )
                copy.start()
                copies.append(copy)
            if not summed:
                own.wait()
            for copy in copies:
                copy.wait()
            if summed:
                total = source(x_ref, me)[...]
                for step in range(1, count):
                    total = total + held[step - 1]
                o_ref[...] = total

        sems = [pltpu.SemaphoreType.DMA((count - 1,)), pltpu.SemaphoreType.DMA((count - 1,))]
        if summed:
            scratch = [pltpu.VMEM((count - 1,) + out_shape, jnp.float32)] + sems
        else:
            scratch = sems + [pltpu.SemaphoreType.DMA]
        return pl.pallas_call(
            kernel,
            out_shape=jax.ShapeDtypeStruct(out_shape, jnp.float32),
            in_specs=[pl.BlockSpec(memory_space=pltpu.VMEM)],
            out_specs=pl.BlockSpec(memory_space=pltpu.VMEM),
            scratch_shapes=scratch,
            compiler_params=pltpu.CompilerParams(
                collective_id=self.calls, has_side_effects=True
            ),
            name=f"panel_{self.calls}",
        )(block)

    @staticmethod
    def columns_of(width):
        return lambda ref, who: ref.at[:, pl.ds(pl.multiple_of(who * width, width), width)]

    @staticmethod
    def block_of(ref, who):
        return ref.at[who]

    @staticmethod
    def whole_of(ref, who):
        return ref

    def to_columns(self, rows_form):
        rows, width = rows_form.shape[0], rows_form.shape[1] // self.count
        got = self.exchange(
            rows_form, (self.count, rows, width), self.columns_of(width), self.block_of, False
        )
        return got.reshape(self.count * rows, width)

    def to_rows(self, columns_form):
        rows, width = columns_form.shape[0] // self.count, columns_form.shape[1]
        return self.exchange(
            columns_form.reshape(self.count, rows, width),
            (rows, self.count * width),
            self.block_of,
            self.columns_of(width),
            False,
        )

    def gather(self, columns_form):
        rows, width = columns_form.shape
        return self.exchange(
            columns_form, (rows, self.count * width), self.whole_of, self.columns_of(width), False
        )

    def sum_to_columns(self, partial):
        rows, width = partial.shape[0], partial.shape[1] // self.count
        return self.exchange(
            partial, (rows, width), self.columns_of(width), self.block_of, True
        )

    def sum_to_rows(self, partial):
        rows, width = partial.shape[0] // self.count, partial.shape[1]
        return self.exchange(
            partial.reshape(self.count, rows, width), (rows, width), self.block_of, self.block_of, True
        )


def selector(chosen, tile_total):
    return (chosen[:, None] == jnp.arange(tile_total, dtype=jnp.int32)[None, :]).astype(jnp.float32)


def local(
    live_tiles, row_tiles, rhs0, rhs1, rhs2, rhs3, dinv0, dinv1, dinv2, dinv3, off0, off1, off2
):
    right_sides = [rhs0, rhs1, rhs2, rhs3]
    inverses = [dinv0, dinv1, dinv2, dinv3]
    off_rows = [off0, off1, off2]
    leaf_index = lax.axis_index("leaf")
    panel_index = lax.axis_index("panel")
    leaf_count = lax.axis_size("leaf")
    panel = Panel()
    panel_count = panel.count
    order_rows = dinv0.shape[0]
    width = dinv0.shape[1]
    tile_count = order_rows // B
    bits = [leaf_index // 2**bit % 2 for bit in range(LEVELS)]
    lower = [bit == 0 for bit in bits]
    first_nodes = []
    start_node = 0
    for height in range(LEVELS):
        first_nodes.append(start_node)
        start_node = start_node + leaf_count // 2**height

    def stacked_rows(block, height):
        shape = block.shape
        for place, bit in enumerate(reversed(range(height))):
            mine = jnp.expand_dims(block, place)
            block = pair(lower[bit], mine, jnp.expand_dims(swapped(block, bit), place), place)
        return block.reshape((shape[0] * 2**height, shape[1]))

    def chosen_of(height, flip):
        node = leaf_index // 2**height
        if flip:
            node = node + 1 - 2 * (node % 2)
        return lax.dynamic_index_in_dim(row_tiles, first_nodes[height] + node, keepdims=False)

    residuals = []
    for height in range(LEVELS):
        block = right_sides[height]
        for bit in range(height):
            got = swapped(pick_half(block, 1 - bits[bit], 0), bit)
            block = pair(lower[bit], pick_half(block, bits[bit], 0), got, 1)
        residuals.append(block)
    for height in range(1, LEVELS):
        inverses[height] = stacked_rows(inverses[height], height)
        if height < LEVELS - 1:
            off_rows[height] = stacked_rows(off_rows[height], height)

    masks = []
    own_masks = []
    for height in range(LEVELS):
        live_count = lax.dynamic_index_in_dim(
            live_tiles, first_nodes[height] + leaf_index // 2**height, keepdims=False
        )
        place = jnp.arange(order_rows, dtype=jnp.int32)
        mask = (place < live_count * B).astype(jnp.float32)[None, :]
        masks.append(mask)
        own_masks.append(lax.dynamic_slice_in_dim(mask, panel_index * width, width, 1))

    sums = None
    kept = []
    for height in range(LEVELS):
        residual = residuals[height]
        if sums is not None:
            residual = residual - sums[:, :order_rows]
            sums = sums[:, order_rows:]
        spread = panel.to_columns(residual * masks[height])
        columns = panel.sum_to_columns(contract_last(spread, inverses[height])) * own_masks[height]
        kept.append(columns)
        if height == LEVELS - 1:
            break
        update = panel.sum_to_rows(contract_last(columns, off_rows[height]))
        span = (LEVELS - 1 - height) * tile_count
        chosen = chosen_of(height, False)
        if sums is None:
            got = swapped(pick_half(update, 1 - bits[height], 0), height)
            update = jnp.concatenate([pick_half(update, bits[height], 0), got], 1)
            chosen = jnp.concatenate([chosen, chosen_of(height, True)])
        pieces = update.reshape(update.shape[0], chosen.shape[0], B)
        sent = jnp.einsum("rtb,tc->rcb", pieces, selector(chosen, span), precision=high)
        sent = sent.reshape(update.shape[0], span * B)
        if sums is None:
            sums = sent
        else:
            sums = sums + sent
            got = swapped(pick_half(sums, 1 - bits[height], 0), height)
            sums = pick_half(sums, bits[height], 0) + got

    outputs = [None] * LEVELS
    known = None
    for height in reversed(range(LEVELS)):
        target = kept[height]
        if known is not None:

            def joined(mine, other):
                rows = mine.shape[0] // panel_count
                shape = (panel_count, rows, mine.shape[1])
                both = pair(lower[height], mine.reshape(shape), other.reshape(shape), 1)
                return both.reshape(2 * mine.shape[0], mine.shape[1])

            span = (LEVELS - 1 - height) * tile_count
            tiles = known.reshape(known.shape[0], span, B)

            def selected(flip):
                picked = selector(chosen_of(height, flip), span)
                found = jnp.einsum("rcb,tc->rtb", tiles, picked, precision=high)
                return found.reshape(known.shape[0], picked.shape[0] * B)

            gathered = joined(selected(False), swapped(selected(True), height))
            target = target - product(gathered, off_rows[height])
            if height > 0:
                known = joined(known, swapped(known, height))
        whole_target = panel.gather(target * own_masks[height])
        solved = product(whole_target, inverses[height]) * own_masks[height]
        if height == 0:
            outputs[0] = panel.to_rows(solved)
            break
        whole = panel.gather(solved)
        rows = whole.shape[0] // panel_count
        known = whole if known is None else jnp.concatenate([whole, known], 1)
        block = lax.dynamic_slice_in_dim(whole, panel_index * rows, rows, 0)
        for bit in reversed(range(height)):
            got = swapped(pick_half(block, 1 - bits[bit], 1), bit)
            block = pair(lower[bit], pick_half(block, bits[bit], 1), got, 0)
        outputs[height] = block
    return tuple(outputs)


def solution(mesh):
    vectors = P("panel", "leaf")
    blocks = P("leaf", "panel")
    return jax.shard_map(
        local,
        mesh=mesh,
        in_specs=(P(), P()) + (vectors,) * 4 + (blocks,) * 7,
        out_specs=(vectors,) * 4,
        check_vma=False,
    )
```

```python
import jax
import jax.numpy as jnp
from jax import lax
from jax.experimental import pallas as pl
from jax.experimental.pallas import tpu as pltpu
from jax.sharding import PartitionSpec as P

B = 128
LEVELS = 4

high = lax.Precision.HIGH


def swapped(block, bit):
    count = lax.axis_size("leaf")
    route = [(low, low ^ (1 << bit)) for low in range(count)]
    return lax.ppermute(block, "leaf", route)


def pair(is_lower, mine, other, axis):
    return jnp.where(
        is_lower, jnp.concatenate([mine, other], axis), jnp.concatenate([other, mine], axis)
    )


def pick_half(array, which, axis):
    half = array.shape[axis] // 2
    return lax.dynamic_slice_in_dim(array, which * half, half, axis)


def contract_last(left, right):
    return lax.dot_general(
        left, right, (((1,), (1,)), ((), ())), precision=high, preferred_element_type=jnp.float32
    )


def product(left, right):
    return jnp.dot(left, right, precision=high, preferred_element_type=jnp.float32)


class Panel:
    def __init__(self):
        self.count = lax.axis_size("panel")
        self.calls = 0

    def exchange(self, block, out_shape, source, target, summed, riders=()):
        count = self.count
        self.calls += 1
        rider_count = len(riders)
        widest = max([2**height for _, height, _, _ in riders], default=1)

        def kernel(x_ref, *rest):
            rider_ins, rest = rest[:rider_count], rest[rider_count:]
            o_ref, rest = rest[0], rest[1:]
            rider_outs, rest = rest[:rider_count], rest[rider_count:]
            if riders:
                rider_sends, rider_recvs = rest[-2:]
                rest = rest[:-2]
            leaf = lax.axis_index("leaf")
            if summed:
                held, send_sems, recv_sems = rest
            else:
                held, (send_sems, recv_sems, local_sem) = o_ref, rest
            me = lax.axis_index("panel")
            barrier = pltpu.get_barrier_semaphore()
            for step in range(1, count):
                pl.semaphore_signal(
                    barrier,
                    inc=1,
                    device_id={"panel": lax.rem(me + step, count)},
                    device_id_type=pl.DeviceIdType.MESH,
                )
            for step in range(1, widest):
                pl.semaphore_signal(
                    barrier,
                    inc=1,
                    device_id={"leaf": leaf - leaf % widest + (leaf + step) % widest},
                    device_id_type=pl.DeviceIdType.MESH,
                )
            if not summed:
                own = pltpu.make_async_copy(source(x_ref, me), target(held, me), local_sem)
                own.start()
            pl.semaphore_wait(barrier, count - 1 + widest - 1)
            copies = []
            for step in sorted(range(1, count), key=lambda s: -min(s, count - s)):
                peer = lax.rem(me + step, count)
                copy = pltpu.make_async_remote_copy(
                    src_ref=source(x_ref, peer),
                    dst_ref=held.at[step - 1] if summed else target(held, me),
                    send_sem=send_sems.at[step - 1],
                    recv_sem=recv_sems.at[step - 1],
                    device_id={"panel": peer},
                    device_id_type=pl.DeviceIdType.MESH,
                )
                copy.start()
                copies.append(copy)
            slot = 0
            for number, (_, height, start, wide) in enumerate(riders):
                group = 2**height
                for step in range(1, group):
                    copy = pltpu.make_async_remote_copy(
                        src_ref=rider_ins[number].at[:, pl.ds(start, wide)],
                        dst_ref=rider_outs[number].at[leaf % group],
                        send_sem=rider_sends.at[slot],
                        recv_sem=rider_recvs.at[slot],
                        device_id={"leaf": leaf - leaf % group + (leaf + step) % group},
                        device_id_type=pl.DeviceIdType.MESH,
                    )
                    copy.start()
                    copies.append(copy)
                    slot += 1
            if not summed:
                own.wait()
            for copy in copies:
                copy.wait()
            if summed:
                total = source(x_ref, me)[...]
                for step in range(1, count):
                    total = total + held[step - 1]
                o_ref[...] = total

        sems = [pltpu.SemaphoreType.DMA((count - 1,)), pltpu.SemaphoreType.DMA((count - 1,))]
        if summed:
            scratch = [pltpu.VMEM((count - 1,) + out_shape, jnp.float32)] + sems
        else:
            scratch = sems + [pltpu.SemaphoreType.DMA]
        slots = sum(2**height - 1 for _, height, _, _ in riders)
        if riders:
            scratch = scratch + [pltpu.SemaphoreType.DMA((slots,)), pltpu.SemaphoreType.DMA((slots,))]
        rider_shapes = [
            jax.ShapeDtypeStruct((2**height, array.shape[0], wide), jnp.float32)
            for array, height, _, wide in riders
        ]
        result = pl.pallas_call(
            kernel,
            out_shape=[jax.ShapeDtypeStruct(out_shape, jnp.float32)] + rider_shapes,
            in_specs=[pl.BlockSpec(memory_space=pltpu.VMEM)]
            + [pl.BlockSpec(memory_space=pl.ANY)] * rider_count,
            out_specs=[pl.BlockSpec(memory_space=pltpu.VMEM)]
            + [pl.BlockSpec(memory_space=pl.ANY)] * rider_count,
            scratch_shapes=scratch,
            compiler_params=pltpu.CompilerParams(
                collective_id=self.calls, has_side_effects=True
            ),
            name=f"panel_{self.calls}",
        )(block, *[array for array, _, _, _ in riders])
        if not riders:
            return result[0]
        leaf = lax.axis_index("leaf")
        whole = []
        for got, (array, height, start, wide) in zip(result[1:], riders):
            mine = array[None, :, start : start + wide]
            full = lax.dynamic_update_slice(got, mine, (leaf % 2**height, 0, 0))
            whole.append(full.reshape(2**height * array.shape[0], wide))
        return result[0], whole

    @staticmethod
    def columns_of(width):
        return lambda ref, who: ref.at[:, pl.ds(pl.multiple_of(who * width, width), width)]

    @staticmethod
    def block_of(ref, who):
        return ref.at[who]

    @staticmethod
    def whole_of(ref, who):
        return ref

    def to_columns(self, rows_form, riders=()):
        rows, width = rows_form.shape[0], rows_form.shape[1] // self.count
        got = self.exchange(
            rows_form, (self.count, rows, width), self.columns_of(width), self.block_of, False, riders
        )
        if riders:
            return got[0].reshape(self.count * rows, width), got[1]
        return got.reshape(self.count * rows, width), []

    def to_rows(self, columns_form):
        rows, width = columns_form.shape[0] // self.count, columns_form.shape[1]
        return self.exchange(
            columns_form.reshape(self.count, rows, width),
            (rows, self.count * width),
            self.block_of,
            self.columns_of(width),
            False,
        )

    def gather(self, columns_form):
        rows, width = columns_form.shape
        return self.exchange(
            columns_form, (rows, self.count * width), self.whole_of, self.columns_of(width), False
        )

    def sum_to_columns(self, partial, riders=()):
        rows, width = partial.shape[0], partial.shape[1] // self.count
        got = self.exchange(
            partial, (rows, width), self.columns_of(width), self.block_of, True, riders
        )
        return got if riders else (got, [])

    def sum_to_rows(self, partial, riders=()):
        rows, width = partial.shape[0] // self.count, partial.shape[1]
        got = self.exchange(
            partial.reshape(self.count, rows, width),
            (rows, width),
            self.block_of,
            self.block_of,
            True,
            riders,
        )
        return got if riders else (got, [])


def selector(chosen, tile_total):
    return (chosen[:, None] == jnp.arange(tile_total, dtype=jnp.int32)[None, :]).astype(jnp.float32)


def local(
    live_tiles, row_tiles, rhs0, rhs1, rhs2, rhs3, dinv0, dinv1, dinv2, dinv3, off0, off1, off2
):
    right_sides = [rhs0, rhs1, rhs2, rhs3]
    off_rows = [off0, off1, off2]
    leaf_index = lax.axis_index("leaf")
    panel_index = lax.axis_index("panel")
    leaf_count = lax.axis_size("leaf")
    panel = Panel()
    panel_count = panel.count
    order_rows = dinv0.shape[0]
    width = dinv0.shape[1]
    tile_count = order_rows // B
    bits = [leaf_index // 2**bit % 2 for bit in range(LEVELS)]
    lower = [bit == 0 for bit in bits]
    first_nodes = []
    start_node = 0
    for height in range(LEVELS):
        first_nodes.append(start_node)
        start_node = start_node + leaf_count // 2**height

    def chosen_of(height, flip):
        node = leaf_index // 2**height
        if flip:
            node = node + 1 - 2 * (node % 2)
        return lax.dynamic_index_in_dim(row_tiles, first_nodes[height] + node, keepdims=False)

    residuals = []
    for height in range(LEVELS):
        block = right_sides[height]
        for bit in range(height):
            got = swapped(pick_half(block, 1 - bits[bit], 0), bit)
            block = pair(lower[bit], pick_half(block, bits[bit], 0), got, 1)
        residuals.append(block)
    parts = 2 if width % (2 * B) == 0 else 1
    part = width // parts
    inverse_parts = [[dinv0], [], [], []]

    masks = []
    own_masks = []
    for height in range(LEVELS):
        live_count = lax.dynamic_index_in_dim(
            live_tiles, first_nodes[height] + leaf_index // 2**height, keepdims=False
        )
        place = jnp.arange(order_rows, dtype=jnp.int32)
        mask = (place < live_count * B).astype(jnp.float32)[None, :]
        masks.append(mask)
        own_masks.append(lax.dynamic_slice_in_dim(mask, panel_index * width, width, 1))

    sums = None
    kept = []
    for height in range(LEVELS):
        residual = residuals[height]
        if sums is not None:
            residual = residual - sums[:, :order_rows]
            sums = sums[:, order_rows:]
        riders = [(off1, 1, 0, width)] if height == 0 else []
        spread, found = panel.to_columns(residual * masks[height], riders)
        if found:
            off_rows[1] = found[0]
        wide = width // len(inverse_parts[height])
        partial = sum(
            contract_last(spread[:, number * wide : (number + 1) * wide], block)
            for number, block in enumerate(inverse_parts[height])
        )
        riders = []
        if height == 0:
            riders = [(dinv1, 1, 0, width), (dinv2, 2, 0, width)]
        if height == 1:
            riders = [(dinv3, 3, 0, part)]
        columns, found = panel.sum_to_columns(partial, riders)
        if height == 0:
            inverse_parts[1], inverse_parts[2] = [found[0]], [found[1]]
        if height == 1:
            inverse_parts[3] = found
        columns = columns * own_masks[height]
        kept.append(columns)
        if height == LEVELS - 1:
            break
        riders = []
        if height == 0:
            riders = [(off2, 2, 0, width)]
        if height == 1 and parts == 2:
            riders = [(dinv3, 3, part, part)]
        update, found = panel.sum_to_rows(contract_last(columns, off_rows[height]), riders)
        if height == 0:
            off_rows[2] = found[0]
        if height == 1:
            inverse_parts[3] = inverse_parts[3] + found
        span = (LEVELS - 1 - height) * tile_count
        chosen = chosen_of(height, False)
        if sums is None:
            got = swapped(pick_half(update, 1 - bits[height], 0), height)
            update = jnp.concatenate([pick_half(update, bits[height], 0), got], 1)
            chosen = jnp.concatenate([chosen, chosen_of(height, True)])
        pieces = update.reshape(update.shape[0], chosen.shape[0], B)
        sent = jnp.einsum("rtb,tc->rcb", pieces, selector(chosen, span), precision=high)
        sent = sent.reshape(update.shape[0], span * B)
        if sums is None:
            sums = sent
        else:
            sums = sums + sent
            got = swapped(pick_half(sums, 1 - bits[height], 0), height)
            sums = pick_half(sums, bits[height], 0) + got

    outputs = [None] * LEVELS
    known = None
    for height in reversed(range(LEVELS)):
        target = kept[height]
        if known is not None:

            def joined(mine, other):
                rows = mine.shape[0] // panel_count
                shape = (panel_count, rows, mine.shape[1])
                both = pair(lower[height], mine.reshape(shape), other.reshape(shape), 1)
                return both.reshape(2 * mine.shape[0], mine.shape[1])

            span = (LEVELS - 1 - height) * tile_count
            tiles = known.reshape(known.shape[0], span, B)

            def selected(flip):
                picked = selector(chosen_of(height, flip), span)
                found = jnp.einsum("rcb,tc->rtb", tiles, picked, precision=high)
                return found.reshape(known.shape[0], picked.shape[0] * B)

            gathered = joined(selected(False), swapped(selected(True), height))
            target = target - product(gathered, off_rows[height])
            if height > 0:
                known = joined(known, swapped(known, height))
        whole_target = panel.gather(target * own_masks[height])
        solved = [product(whole_target, block) for block in inverse_parts[height]]
        solved = jnp.concatenate(solved, 1) * own_masks[height]
        if height == 0:
            outputs[0] = panel.to_rows(solved)
            break
        whole = panel.gather(solved)
        rows = whole.shape[0] // panel_count
        known = whole if known is None else jnp.concatenate([whole, known], 1)
        block = lax.dynamic_slice_in_dim(whole, panel_index * rows, rows, 0)
        for bit in reversed(range(height)):
            got = swapped(pick_half(block, 1 - bits[bit], 1), bit)
            block = pair(lower[bit], pick_half(block, bits[bit], 1), got, 0)
        outputs[height] = block
    return tuple(outputs)


def solution(mesh):
    vectors = P("panel", "leaf")
    blocks = P("leaf", "panel")
    return jax.shard_map(
        local,
        mesh=mesh,
        in_specs=(P(), P()) + (vectors,) * 4 + (blocks,) * 7,
        out_specs=(vectors,) * 4,
        check_vma=False,
    )
```
